128 devices in a mesh: slab: 4 (over z), brick: 32 (over y, x, core).
Axes of the slice: x: 4, y: 4, z: 4, core: 2. Of those that a mesh axis runs over, the one named last changes fastest.
Arguments:
- positions: float32 [4, 3, 65536], P('slab', None, 'brick'), may hold values from 0 to 1
- dest_brick: int32 [4, 65536], P('slab', 'brick'), may hold values from 0 to 31, as said below
- cell_local: int32 [4, 65536], P('slab', 'brick'), may hold values from 0 to 31
Outputs:
- rebuilt: float32 [4, 7, 65536], P('slab', None, 'brick')
The draws below stay inside these ranges and needn't reach their ends.
Inputs may be any that keep to these rules, and one draw needn't show every extreme that they name: `dest_brick`: an atom held by brick b (columns b * 2048 to (b + 1) * 2048 - 1) goes to brick b, b + 1 or b - 1, periodic along the bricks. Of one brick's atoms at most 112 stay in one of its own cells and at most 8 go to one cell of each brick beside it; in every brick some cell receives exactly these numbers from all three, 128 atoms.
All inputs are finite; a program needn't handle non-finite values.
Results may differ from the reference program's by a relative error of at most 0.0003.
Values sent between devices are 32-bit elements; how exact they have to be, the bound alone decides.
A program may use at most 64 MiB of HBM per device.

```python
import jax
import jax.numpy as jnp
from jax import lax

CX = 1
CY = 8
CZ = 4
CAP = 128
SIDE_MOST = 8
OWN_MOST = 112
CELLS_DEV = 32
ATOM_DEV = 2048
ATOMS_ROW = 65536
N_SLAB = 4
N_BRICK = 32


def route_table(key):
    device_total = N_SLAB * N_BRICK
    slot_count = CELLS_DEV * CAP
    own_span = CELLS_DEV * OWN_MOST
    side_span = CELLS_DEV * SIDE_MOST
    full_cell = jax.random.randint(jax.random.fold_in(key, 11), (N_SLAB, N_BRICK), 0, CELLS_DEV)
    right_full = jnp.roll(full_cell, -1, axis=1)
    left_full = jnp.roll(full_cell, 1, axis=1)
    slot_ids = jnp.arange(slot_count, dtype=jnp.int32)
    relative = jnp.where(slot_ids < own_span, 0, jnp.where(slot_ids < own_span + side_span, 1, -1))
    cell_ids = jnp.where(slot_ids < own_span, slot_ids // OWN_MOST, jnp.where(slot_ids < own_span + side_span, (slot_ids - own_span) // SIDE_MOST, (slot_ids - own_span - side_span) // SIDE_MOST))
    wanted = jnp.where(relative[None, None, :] == 0, full_cell[..., None], jnp.where(relative[None, None, :] == 1, right_full[..., None], left_full[..., None]))
    forced = cell_ids[None, None, :] == wanted
    device_keys = jax.random.split(jax.random.fold_in(key, 12), device_total)
    random_rank = jax.vmap(lambda subkey: jax.random.permutation(subkey, slot_count))(device_keys)
    random_rank = random_rank.reshape(N_SLAB, N_BRICK, slot_count).astype(jnp.int32)
    scores = jnp.where(forced, slot_ids[None, None, :] - slot_count, random_rank)
    chosen = jnp.argsort(scores, axis=-1)[..., :ATOM_DEV]
    shuffle_keys = jax.random.split(jax.random.fold_in(key, 13), device_total)
    shuffle = jax.vmap(lambda subkey: jax.random.permutation(subkey, ATOM_DEV))(shuffle_keys)
    shuffle = shuffle.reshape(N_SLAB, N_BRICK, ATOM_DEV)
    picked = jnp.take_along_axis(chosen, shuffle, axis=-1)
    bricks = jnp.arange(N_BRICK, dtype=jnp.int32)[None, :, None]
    destination = (bricks + relative[picked]) % N_BRICK
    return (destination.reshape(N_SLAB, N_BRICK * ATOM_DEV).astype(jnp.int32), cell_ids[picked].reshape(N_SLAB, N_BRICK * ATOM_DEV).astype(jnp.int32))


def draw_dest_brick(key, part):
    return route_table(key)[0]


def draw_cell_local(key, part):
    return route_table(key)[1]


def steps_of(stream_key, shape, pieces, low, top_value):
    loudness = 1.0
    for axis_at, blocks in pieces:
        steps = jax.random.uniform(jax.random.fold_in(jax.random.fold_in(stream_key, 6), axis_at), (blocks,), jnp.float32, low / len(pieces), top_value / len(pieces))
        loudness = loudness * jnp.repeat(jnp.exp(steps), shape[axis_at] // blocks).reshape((-1,) + (1,) * (len(shape) - 1 - axis_at))
    return loudness


def setup_inputs(seed: int = 0) -> dict:
    key_list = jax.random.split(jax.random.key(seed), 4)
    return {
        "positions": jnp.clip(1.0 * jax.random.uniform(key_list[0], (N_SLAB, 3, ATOMS_ROW), jnp.float32) ** steps_of(key_list[0], (N_SLAB, 3, ATOMS_ROW), ((0, 4), (2, 32)), -0.2, 0.2), 0.0, 1.0),
        "dest_brick": draw_dest_brick(jax.random.fold_in(key_list[3], 71), 0),
        "cell_local": draw_cell_local(jax.random.fold_in(key_list[3], 71), 0),
    }


SIGMA_SQ = 0.8
SOFT_SQ = 0.64
EPSILON = 0.05
SENTINEL = 64.0


def pair_sums(own_cell, other_cell, offset, self_pair):
    delta_x = own_cell[0][..., :, None] - (other_cell[0][..., None, :] + offset[0])
    delta_y = own_cell[1][..., :, None] - (other_cell[1][..., None, :] + offset[1])
    delta_z = own_cell[2][..., :, None] - (other_cell[2][..., None, :] + offset[2])
    dist_sq = delta_x * delta_x + delta_y * delta_y + delta_z * delta_z
    inverse = 1.0 / (dist_sq + SOFT_SQ)
    ratio = SIGMA_SQ * inverse
    cube_term = ratio * ratio * ratio
    sixth_term = cube_term * cube_term
    well_value = 4.0 * (sixth_term - cube_term)
    slope_value = -4.0 * (6.0 * sixth_term - 3.0 * cube_term) * inverse
    margin = jnp.maximum(1.0 - dist_sq, 0.0)
    energy = well_value * margin * margin
    derive = slope_value * margin * margin - 2.0 * well_value * margin
    if self_pair:
        distinct = lax.broadcasted_iota(jnp.int32, (CAP, CAP), 0) != lax.broadcasted_iota(jnp.int32, (CAP, CAP), 1)
        energy = jnp.where(distinct, energy, 0.0)
        derive = jnp.where(distinct, derive, 0.0)
    factor = -2.0 * EPSILON * derive
    return jnp.stack([jnp.sum(factor * delta_x, -1), jnp.sum(factor * delta_y, -1),
                      jnp.sum(factor * delta_z, -1), 0.5 * EPSILON * jnp.sum(energy, -1)])


def cell_forces(cell_grid):
    padded = jnp.pad(cell_grid, ((0, 0), (1, 1), (1, 1), (1, 1), (0, 0)), mode="wrap")
    width_y = cell_grid.shape[2]
    width_z = cell_grid.shape[3]

    def one_plane(plane_index):
        own_cell = lax.dynamic_index_in_dim(cell_grid, plane_index, 1, keepdims=False)
        running = jnp.zeros((4, width_y, width_z, CAP), cell_grid.dtype)
        for step_x in (-1, 0, 1):
            near_plane = lax.dynamic_index_in_dim(padded, plane_index + 1 + step_x, 1, keepdims=False)
            for step_y in (-1, 0, 1):
                for step_z in (-1, 0, 1):
                    other_cell = near_plane[:, 1 + step_y:1 + step_y + width_y, 1 + step_z:1 + step_z + width_z]
                    running = running + pair_sums(own_cell, other_cell, (float(step_x), float(step_y), float(step_z)),
                                                  step_x == 0 and step_y == 0 and step_z == 0)
        return running

    return lax.map(one_plane, jnp.arange(cell_grid.shape[1], dtype=jnp.int32))


def reference(positions, dest_brick, cell_local):
    columns = jnp.arange(ATOMS_ROW, dtype=jnp.int32)
    source = columns // ATOM_DEV
    cell_grid = jnp.full((3, N_BRICK * CX, CY, N_SLAB * CZ, CAP), SENTINEL, positions.dtype)
    placed = []
    for slab_id in range(N_SLAB):
        target = dest_brick[slab_id].astype(jnp.int32)
        differ = (target - source) % N_BRICK
        group_id = jnp.where(differ == N_BRICK - 1, 2, differ)
        cell_key = target * CELLS_DEV + cell_local[slab_id].astype(jnp.int32)
        ranking = jnp.argsort(cell_key * 3 + group_id, stable=True)
        sorted_key = cell_key[ranking]
        tallies = jax.ops.segment_sum(jnp.ones_like(cell_key), cell_key, num_segments=N_BRICK * CELLS_DEV)
        starts = jnp.cumsum(tallies) - tallies
        slot_id = columns - starts[sorted_key]
        local_cell = sorted_key % CELLS_DEV
        grid_x = (sorted_key // CELLS_DEV) * CX + local_cell // (CY * CZ)
        grid_y = (local_cell // CZ) % CY
        grid_z = slab_id * CZ + local_cell % CZ
        moved_pos = positions[slab_id][:, ranking]
        cell_grid = cell_grid.at[:, grid_x, grid_y, grid_z, slot_id].set(moved_pos)
        placed.append((moved_pos, grid_x, grid_y, grid_z, slot_id))
    slot_terms = cell_forces(cell_grid)
    rows_out = []
    for moved_pos, grid_x, grid_y, grid_z, slot_id in placed:
        picked = slot_terms[grid_x, :, grid_y, grid_z, slot_id].T
        rows_out.append(jnp.concatenate([moved_pos, picked], axis=0))
    return jnp.stack(rows_out)
```

```python
import math

import jax
import jax.numpy as jnp
from jax import lax
from jax.sharding import PartitionSpec as P

CX = 1
CY = 8
CZ = 4
CAP = 128
SIDE_MOST = 8
CELLS_DEV = 32


SIGMA_SQ = 0.8
SOFT_SQ = 0.64
EPSILON = 0.05
SENTINEL = 64.0


def passed_along(value, axis, steps):
    count = lax.axis_size(axis)
    pairs = [(source, (source + steps) % count) for source in range(count)]
    return lax.ppermute(value, axis, pairs)


def extended(block, sides, width):
    for axis, dim in sides:
        count = lax.axis_size(axis)
        forward = [(i, i + 1) for i in range(count - 1)]
        forward.append((count - 1, 0))
        backward = [(target, source) for source, target in forward]
        low = lax.ppermute(
            lax.slice_in_dim(block, block.shape[dim] - width, None, axis=dim), axis, forward
        )
        high = lax.ppermute(lax.slice_in_dim(block, 0, width, axis=dim), axis, backward)
        block = jnp.concatenate([low, block, high], axis=dim)
    return block


def prefix(shard, axis, combine, identity):
    mine = lax.axis_index(axis)
    everything = lax.all_gather(shard, axis)
    lower = jnp.arange(everything.shape[0], dtype=jnp.int32) < mine
    return jnp.sum(jnp.where(lower, everything, identity))


def from_behind(block, axis, distance):
    devices = range(lax.axis_size(axis))
    route = [(i - distance, i) for i in devices if i - distance in devices]
    return lax.ppermute(block, axis, route)


def pair_sums(own_cell, other_cell, offset, self_pair):
    delta_x = own_cell[0][..., :, None] - (other_cell[0][..., None, :] + offset[0])
    delta_y = own_cell[1][..., :, None] - (other_cell[1][..., None, :] + offset[1])
    delta_z = own_cell[2][..., :, None] - (other_cell[2][..., None, :] + offset[2])
    dist_sq = delta_x * delta_x + delta_y * delta_y + delta_z * delta_z
    inverse = 1.0 / (dist_sq + SOFT_SQ)
    ratio = SIGMA_SQ * inverse
    cube_term = ratio * ratio * ratio
    sixth_term = cube_term * cube_term
    well_value = 4.0 * (sixth_term - cube_term)
    slope_value = -4.0 * (6.0 * sixth_term - 3.0 * cube_term) * inverse
    margin = jnp.maximum(1.0 - dist_sq, 0.0)
    energy = well_value * margin * margin
    derive = slope_value * margin * margin - 2.0 * well_value * margin
    if self_pair:
        distinct = lax.broadcasted_iota(jnp.int32, (CAP, CAP), 0) != lax.broadcasted_iota(
            jnp.int32, (CAP, CAP), 1
        )
        energy = jnp.where(distinct, energy, 0.0)
        derive = jnp.where(distinct, derive, 0.0)
    factor = -2.0 * EPSILON * derive
    return jnp.stack(
        [
            jnp.sum(factor * delta_x, -1),
            jnp.sum(factor * delta_y, -1),
            jnp.sum(factor * delta_z, -1),
            0.5 * EPSILON * jnp.sum(energy, -1),
        ]
    )


def group_ranks(group_key, groups):
    row_count = group_key.shape[0]
    block_rows = math.gcd(row_count, 256)
    row_iota = lax.broadcasted_iota(jnp.int32, (block_rows, block_rows), 0)
    lower_ones = (row_iota > lax.broadcasted_iota(jnp.int32, (block_rows, block_rows), 1)).astype(
        jnp.bfloat16
    )
    labels = jnp.arange(groups, dtype=jnp.int32)

    def advance(counts, key_block):
        matches = key_block[:, None] == labels[None, :]
        one_hot = matches.astype(jnp.bfloat16)
        within = jnp.dot(lower_ones, one_hot, preferred_element_type=jnp.float32)
        ranked = jnp.sum(jnp.where(matches, within + counts[None, :], 0.0), axis=1)
        return (counts + jnp.sum(one_hot, axis=0, dtype=jnp.float32), ranked.astype(jnp.int32))

    counts, ranked = lax.scan(
        advance, jnp.zeros((groups,), jnp.float32), group_key.reshape(-1, block_rows)
    )
    return (ranked.reshape(row_count), counts.astype(jnp.int32))


def add_counts(earlier, later):
    return earlier + later


def place_rows(result, rows_in, first_global, count_rows, shard_first):
    column_ids = jnp.arange(rows_in.shape[1], dtype=jnp.int32)
    target_col = first_global + column_ids - shard_first
    usable = (column_ids < count_rows) & (target_col >= 0) & (target_col < result.shape[1])
    return result.at[:, jnp.where(usable, target_col, result.shape[1])].set(rows_in, mode="drop")


def body(positions, dest_brick, cell_local):
    brick_count = lax.axis_size("brick")
    brick_index = lax.axis_index("brick")
    atom_place = positions[0]
    target = dest_brick[0]
    cell_of = cell_local[0]
    atom_count = target.shape[0]
    side_slots = CELLS_DEV * SIDE_MOST
    grid_slots = CELLS_DEV * CAP
    bucket = (target - brick_index + 1) % brick_count
    slot_rank, counts = group_ranks(bucket * CELLS_DEV + cell_of, 3 * CELLS_DEV)
    own_counts = counts[CELLS_DEV : 2 * CELLS_DEV]

    def outgoing(bucket_id):
        slot_index = jnp.where(bucket == bucket_id, cell_of * SIDE_MOST + slot_rank, side_slots)
        return (
            jnp.full((3, side_slots), SENTINEL, jnp.float32)
            .at[:, slot_index]
            .set(atom_place, mode="drop")
        )

    from_left = passed_along(outgoing(2), "brick", 1)
    from_right = passed_along(outgoing(0), "brick", -1)
    own_index = jnp.where(bucket == 1, cell_of * CAP + slot_rank, grid_slots)
    cell_grid = (
        jnp.full((3, grid_slots), SENTINEL, jnp.float32)
        .at[:, own_index]
        .set(atom_place, mode="drop")
    )
    side_iota = jnp.arange(SIDE_MOST, dtype=jnp.int32)[None, :]
    cell_base = jnp.arange(CELLS_DEV, dtype=jnp.int32)[:, None] * CAP

    def arrive(grid_now, arrived, before):
        present = arrived[0].reshape(CELLS_DEV, SIDE_MOST) < 2.0
        landing = jnp.where(present, cell_base + before[:, None] + side_iota, grid_slots).reshape(
            -1
        )
        return (
            grid_now.at[:, landing].set(arrived, mode="drop"),
            jnp.sum(present.astype(jnp.int32), axis=1),
        )

    cell_grid, left_counts = arrive(cell_grid, from_left, own_counts)
    cell_grid, right_counts = arrive(cell_grid, from_right, own_counts + left_counts)
    cell_counts = own_counts + left_counts + right_counts
    padded = extended(cell_grid.reshape(3, CX, CY, CZ, CAP), (("slab", 3), ("brick", 1)), 1)

    def column_forces(column, running):
        place_x = column // CY
        place_y = column % CY
        own_cell = lax.dynamic_slice(padded, (0, place_x + 1, place_y, 1, 0), (3, 1, 1, CZ, CAP))[
            :, 0, 0
        ]
        summed = jnp.zeros((4, CZ, CAP), jnp.float32)
        for step_x in (-1, 0, 1):
            for step_y in (-1, 0, 1):
                near_y = (place_y + step_y) % CY
                for step_z in (-1, 0, 1):
                    other_cell = lax.dynamic_slice(
                        padded, (0, place_x + 1 + step_x, near_y, 1 + step_z, 0), (3, 1, 1, CZ, CAP)
                    )[:, 0, 0]
                    summed = summed + pair_sums(
                        own_cell,
                        other_cell,
                        (float(step_x), float(step_y), float(step_z)),
                        step_x == 0 and step_y == 0 and (step_z == 0),
                    )
        return lax.dynamic_update_slice(running, summed[:, None], (0, column, 0, 0))

    slot_terms = lax.fori_loop(
        0, CX * CY, column_forces, jnp.zeros((4, CX * CY, CZ, CAP), jnp.float32)
    )
    slot_terms = slot_terms.reshape(4, grid_slots)
    cell_start = jnp.cumsum(cell_counts) - cell_counts
    kept_total = jnp.sum(cell_counts)
    slot_iota = jnp.arange(CAP, dtype=jnp.int32)[None, :]
    filled = slot_iota < cell_counts[:, None]
    packed_index = jnp.where(filled, cell_start[:, None] + slot_iota, grid_slots).reshape(-1)
    records = jnp.concatenate([cell_grid, slot_terms], axis=0)
    packed = jnp.zeros((7, grid_slots), jnp.float32).at[:, packed_index].set(records, mode="drop")
    first_row = prefix(kept_total, "brick", add_counts, jnp.int32(0))
    shard_first = brick_index * atom_count
    result = place_rows(
        jnp.zeros((7, atom_count), jnp.float32), packed, first_row, kept_total, shard_first
    )
    summary = jnp.stack([first_row, kept_total]).astype(jnp.float32)
    left_rows, left_summary = from_behind((packed, summary), "brick", 1)
    right_rows, right_summary = from_behind((packed, summary), "brick", -1)
    result = place_rows(
        result,
        left_rows,
        left_summary[0].astype(jnp.int32),
        left_summary[1].astype(jnp.int32),
        shard_first,
    )
    result = place_rows(
        result,
        right_rows,
        right_summary[0].astype(jnp.int32),
        right_summary[1].astype(jnp.int32),
        shard_first,
    )
    return result[None]


def solution(mesh):
    return jax.shard_map(
        body,
        mesh=mesh,
        in_specs=(P("slab", None, "brick"), P("slab", "brick"), P("slab", "brick")),
        out_specs=P("slab", None, "brick"),
        check_vma=False,
    )
```
